32 devices in a mesh: tile: 8 (over y, x, core), grp: 4 (over z).
Axes of the slice: x: 2, y: 2, z: 4, core: 2. Of those that a mesh axis runs over, the one named last changes fastest.
Arguments:
- amplitudes: bfloat16 [2, 64, 4096], P(None, 'tile', 'grp'), may hold values from -6 to 6
- integrals: bfloat16 [8, 16, 256, 256], P('tile', 'grp'), may hold values from -0.1875 to 0.1875
- slot_cd: int32 [8, 16], P('tile'), may hold values from 0 to 3
- slot_ab: int32 [8, 16], P('tile'), may hold values from 0 to 2, as said below
Outputs:
- ladder: bfloat16 [2, 64, 4096], P(None, 'grp', 'tile')
The draws below stay inside these ranges and needn't reach their ends.
Inputs may be any that keep to these rules, and one draw needn't show every extreme that they name: `slot_ab`: 2 marks an empty slot. In every grid column one index of grp has all of its 4 slots live.
All inputs are finite; a program needn't handle non-finite values.
Results may differ from the reference program's by a relative error of at most 0.0085.
Values may be sent and summed in bfloat16 or wider, within the bound.
A program may use at most 64 MiB of HBM per device.

```python
import jax
import jax.numpy as jnp
from jax import lax

TW = 256
NT_DEV = 2
BATCH = 2
PAIRS = 64
NT = 16
CT = 4
N_TILE = 8
N_GRP = 4


def live_table(key):
    groups = N_GRP
    key_busy, key_load, key_offset = jax.random.split(jax.random.fold_in(key, 11), 3)
    busiest = jax.random.randint(key_busy, (N_TILE,), 0, groups)
    loads = jax.random.randint(key_load, (N_TILE, groups), 1, max(groups // 3, 1) + 1)
    device_ids = jnp.arange(groups, dtype=jnp.int32)
    loads = jnp.where(device_ids[None, :] == busiest[:, None], groups, loads)
    offsets = jax.random.randint(key_offset, (N_TILE, groups), 0, groups)
    slot_ids = jnp.arange(groups, dtype=jnp.int32)
    shifted = (slot_ids[None, None, :] - offsets[:, :, None]) % groups
    return (shifted < loads[:, :, None]).reshape(N_TILE, groups * groups)


def draw_slot_ab(key, part):
    live = live_table(key)
    chosen = jax.random.randint(jax.random.fold_in(key, 7), (N_TILE, N_GRP * N_GRP), 0, NT_DEV)
    return jnp.where(live, chosen, NT_DEV).astype(jnp.int32)


def touch_ends(entries, key, least, high):
    longest = entries.shape.index(max(entries.shape))
    spots = []
    for shift in (0, 1):
        where = [jax.random.randint(jax.random.fold_in(key, axis), (), 0, length) for axis, length in enumerate(entries.shape)]
        where[longest] = (where[longest] + shift) % entries.shape[longest]
        spots.append(tuple(where))
    return entries.at[spots[0]].set(least).at[spots[1]].set(high)


def levels(key, dims, shards, smallest, high):
    def one(axis_at, blocks):
        heights = jax.random.uniform(jax.random.fold_in(jax.random.fold_in(key, 6), axis_at), (blocks,), jnp.float32, smallest / len(shards), high / len(shards))
        return jnp.repeat(jnp.exp(heights), dims[axis_at] // blocks).reshape((-1,) + (1,) * (len(dims) - axis_at - 1))

    gain = one(*shards[0])
    for cut in shards[1:]:
        gain = gain * one(*cut)
    return gain


def centred(key, shape, scale, bound, cuts=(), kind=jnp.bfloat16):
    loudness = levels(key, shape, cuts, -0.22, 0.18) if cuts else 1.0
    array = jax.random.normal(key, shape, jnp.float32) * scale * loudness
    return jnp.minimum(jnp.maximum(array, -bound), bound).astype(kind)


def setup_inputs(seed: int = 0) -> dict:
    key_list = jax.random.split(jax.random.key(seed), 5)
    return {
        "amplitudes": centred(key_list[0], (BATCH, PAIRS, NT * TW), 1.0, 6.0, ((1, 8), (2, 4))),
        "integrals": centred(key_list[1], (N_TILE, N_GRP * N_GRP, TW, TW), (TW * N_GRP) ** -0.5, 0.1875, ((0, 8), (1, 4))),
        "slot_cd": touch_ends(jax.random.randint(key_list[2], (N_TILE, N_GRP * N_GRP), 0, CT), jax.random.fold_in(key_list[2], 1), 0, CT - 1).astype(jnp.int32),
        "slot_ab": draw_slot_ab(jax.random.fold_in(key_list[4], 71), 0),
    }


def column_block(amplitudes, column_tiles, cd_list, ab_list):
    owners = jnp.arange(N_GRP * N_GRP, dtype=jnp.int32) % N_GRP
    global_cd = (owners * CT + cd_list).astype(jnp.int32)
    tiled = amplitudes.reshape(BATCH, PAIRS, NT, TW)
    picked = jnp.take(tiled, global_cd, axis=2).astype(jnp.float32)
    products = jnp.einsum("bpsc,scd->bpsd", picked, column_tiles.astype(jnp.float32))
    select = (ab_list[:, None] == jnp.arange(NT_DEV, dtype=jnp.int32)[None, :]).astype(jnp.float32)
    summed = jnp.einsum("bpsd,sa->bpad", products, select)
    return summed.reshape(BATCH, PAIRS, NT_DEV * TW)


def reference(amplitudes, integrals, slot_cd, slot_ab):
    def one_column(operands):
        return column_block(amplitudes, operands[0], operands[1], operands[2])

    columns = lax.map(one_column, (integrals, slot_cd, slot_ab))
    ladder = 0.5 * jnp.transpose(columns, (1, 2, 0, 3)).reshape(BATCH, PAIRS, NT * TW)
    return ladder.astype(jnp.bfloat16)
```

```python
import functools

import jax
import jax.numpy as jnp
from jax import lax
from jax.experimental import pallas as pl
from jax.experimental.pallas import tpu as pltpu
from jax.sharding import PartitionSpec as P

MESH = pl.DeviceIdType.MESH
NT_DEV = 2
BATCH = 2
GATHER_LIMIT = 8 * 2**20
CORES = 2


def flip(index, mask):
    bit = 1
    while bit <= mask:
        if mask & bit:
            index = index + bit * (1 - 2 * lax.rem(lax.div(index, jnp.int32(bit)), jnp.int32(2)))
        bit *= 2
    return index


def farthest_first(own, count):
    low, high = jnp.int32(0), jnp.int32(count - 1)
    order = []
    for _ in range(count - 1):
        take_low = (own - low >= high - own).astype(jnp.int32)
        order.append(take_low * low + (1 - take_low) * high)
        low, high = low + take_low, high - (1 - take_low)
    return order


def kernel(groups, places, amp_ref, int_ref, cd_ref, ab_ref, out_ref, zbuf, xbuf, pbuf, abuf, sbuf, tile_buf, acc, rs_buf,
           sums_buf, cd_smem, ab_smem, amp_sem, local_sem, z_send, z_recv, t_send, t_recv, p_send, p_recv, x_send, x_recv,
           a_send, a_recv, rs_send, rs_recv):
    g, t = lax.axis_index("grp"), lax.axis_index("tile")
    place, core = lax.div(t, jnp.int32(CORES)), lax.rem(t, jnp.int32(CORES))
    widths = int_ref.shape[-1]
    tiles_dev = zbuf.shape[1]
    near = places * CORES
    spot = [flip(place, q) for q in range(places)]
    column = [spot[e // CORES] * CORES + (1 - core if e % CORES else core) for e in range(near)]
    order = farthest_first(g, groups)

    barrier = pltpu.get_barrier_semaphore()
    peers = [(t, order[k]) for k in range(groups - 1)] + [(column[e], g) for e in range(1, near)]
    for peer in peers:
        pl.semaphore_signal(barrier, inc=1, device_id=peer, device_id_type=MESH)
    amp_copies = [
        pltpu.make_async_copy(amp_ref.at[:, :, pl.ds(c * widths, widths)], zbuf.at[g, c], amp_sem.at[c])
        for c in range(tiles_dev)
    ]
    cd_copy = pltpu.make_async_copy(cd_ref, cd_smem.at[0], local_sem.at[0])
    ab_copy = pltpu.make_async_copy(ab_ref, ab_smem, local_sem.at[1])
    int_copy = pltpu.make_async_copy(int_ref, tile_buf, local_sem.at[2])
    for copy in (cd_copy, *amp_copies, ab_copy, int_copy):
        copy.start()
    pl.semaphore_wait(barrier, len(peers))

    def remote(src, dst, send, recv, peer):
        return pltpu.make_async_remote_copy(
            src_ref=src, dst_ref=dst, send_sem=send, recv_sem=recv, device_id=peer, device_id_type=MESH)

    started = []

    def send(*what):
        copy = remote(*what)
        copy.start()
        started.append(copy)
        return copy

    cd_copy.wait()
    tables = [
        send(cd_smem.at[0], cd_smem.at[e], t_send.at[e - 1], t_recv.at[e - 1], (column[e], g)) for e in range(1, near)
    ]
    for copy in amp_copies:
        copy.wait()
    for k in range(groups - 1):
        send(zbuf.at[g], zbuf.at[g], z_send.at[k], z_recv.at[g], (t, order[k]))
    blocks = [
        send(zbuf.at[g], pbuf.at[e - 1], p_send.at[e - 1], p_recv.at[e - 1], (column[e], g)) for e in range(1, near)
    ]
    ab_copy.wait()
    int_copy.wait()

    def choose(tiles, e, j):
        cd = cd_smem[e, 0, g * groups + j]
        chosen = tiles[0]
        for c in range(1, len(tiles)):
            chosen = jnp.where(cd == c, tiles[c], chosen)
        return chosen

    def load(buf, at):
        return [buf[at, c] for c in range(tiles_dev)]

    def term(parts, j):
        operand = jnp.concatenate([part.reshape(-1, widths) for part in parts], axis=0)
        product = jnp.dot(operand, tile_buf[0, j], preferred_element_type=jnp.float32)
        ab = ab_smem[0, g * groups + j]
        return [product * (ab == a).astype(jnp.float32) for a in range(NT_DEV)]

    def add(left, right):
        return [x + y for x, y in zip(left, right)]

    def finish(q, totals):
        for a in range(NT_DEV):
            acc[q, :, a * widths:(a + 1) * widths] = totals[a]
            rs_buf[q, :, a * widths:(a + 1) * widths] = totals[a].astype(rs_buf.dtype)

        @pl.when(spot[q] != g)
        def _():
            remote(rs_buf.at[q], sums_buf.at[g], rs_send.at[q], rs_recv.at[g], (t, spot[q])).start()

    blocks[0].wait_recv()
    own = term([choose(load(zbuf, g), 0, g), choose(load(pbuf, 0), 0, g)], g)
    for copy in tables:
        copy.wait_recv()
    crossings, picked = [], [[] for _ in range(places)]
    for k in range(groups - 1):
        j = order[k]
        remote(zbuf.at[j], zbuf.at[j], z_send.at[k], z_recv.at[j], (t, j)).wait_recv()
        crossings.append(send(zbuf.at[j], xbuf.at[k], x_send.at[k], x_recv.at[k], (column[1], g)))
        arrived = load(zbuf, j)
        for e in range(CORES, near):
            sbuf[k, e - CORES] = choose(arrived, e, j)
        for e in range(CORES, near):
            at = e - CORES
            picked[e // CORES].append(
                send(sbuf.at[k, at], abuf.at[k, at], a_send.at[k, at], a_recv.at[k, at], (column[e], g)))
    for k in range(groups - 1):
        crossings[k].wait_recv()
        j = order[k]
        own = add(own, term([choose(load(zbuf, j), 0, j), choose(load(xbuf, k), 0, j)], j))
    finish(0, own)
    for q in range(1, places):
        for r in range(CORES):
            blocks[q * CORES + r - 1].wait_recv()
        totals = term([choose(load(pbuf, q * CORES + r - 1), 0, g) for r in range(CORES)], g)
        for k in range(groups - 1):
            for r in range(CORES):
                picked[q][k * CORES + r].wait_recv()
            totals = add(totals, term([abuf[k, (q - 1) * CORES + r] for r in range(CORES)], order[k]))
        finish(q, totals)

    mine = jnp.int32(0)
    for q in range(places):
        mine = mine + q * (spot[q] == g).astype(jnp.int32)
    total = acc[mine]
    for k in range(groups - 1):
        j = order[k]
        remote(sums_buf.at[j], sums_buf.at[j], rs_send.at[0], rs_recv.at[j], (t, j)).wait_recv()
        total = total + sums_buf[j].astype(jnp.float32)
    total = (0.5 * total).astype(out_ref.dtype)
    half = total.shape[0] // CORES
    shape = (out_ref.shape[0], out_ref.shape[1] // CORES, out_ref.shape[2])
    same, other = total[:half].reshape(shape), total[half:].reshape(shape)
    first = core == 0
    out_ref[:, :shape[1], :] = jnp.where(first, same, other)
    out_ref[:, shape[1]:, :] = jnp.where(first, other, same)
    for copy in started:
        copy.wait_send()
    for q in range(places):
        @pl.when(spot[q] != g)
        def _():
            remote(rs_buf.at[q], sums_buf.at[g], rs_send.at[q], rs_recv.at[g], (t, spot[q])).wait_send()


def fused(groups, tiles, amplitudes, integrals, slot_cd, slot_ab):
    batch, pairs_dev, span = amplitudes.shape
    widths = integrals.shape[-1]
    places = tiles // CORES
    rows = pairs_dev * tiles // groups
    result = NT_DEV * widths
    tiles_dev = span // widths
    hbm = pl.BlockSpec(memory_space=pltpu.HBM)
    block = (tiles_dev, batch, pairs_dev, widths)
    piece = CORES * batch * pairs_dev
    others, around = groups - 1, CORES * (places - 1)
    dma = pltpu.SemaphoreType.DMA
    return pl.pallas_call(
        functools.partial(kernel, groups, places),
        out_shape=jax.ShapeDtypeStruct((batch, rows, result), jnp.bfloat16),
        in_specs=[hbm] * 4,
        out_specs=pl.BlockSpec(memory_space=pltpu.VMEM),
        scratch_shapes=[
            pltpu.VMEM((groups, *block), jnp.bfloat16),
            pltpu.VMEM((others, *block), jnp.bfloat16),
            pltpu.VMEM((tiles - 1, *block), jnp.bfloat16),
            pltpu.VMEM((others, around, batch, pairs_dev, widths), jnp.bfloat16),
            pltpu.VMEM((others, around, batch, pairs_dev, widths), jnp.bfloat16),
            pltpu.VMEM(integrals.shape, jnp.bfloat16),
            pltpu.VMEM((places, piece, result), jnp.float32),
            pltpu.VMEM((places, piece, result), jnp.bfloat16),
            pltpu.VMEM((groups, piece, result), jnp.bfloat16),
            pltpu.SMEM((tiles, *slot_cd.shape), jnp.int32),
            pltpu.SMEM(slot_ab.shape, jnp.int32),
            dma((tiles_dev,)),
            dma((3,)),
            dma((others,)),
            dma((groups,)),
            dma((tiles - 1,)),
            dma((tiles - 1,)),
            dma((tiles - 1,)),
            dma((tiles - 1,)),
            dma((others,)),
            dma((others,)),
            dma((others, around)),
            dma((others, around)),
            dma((places,)),
            dma((groups,)),
        ],
        compiler_params=pltpu.CompilerParams(collective_id=0, has_side_effects=True, vmem_limit_bytes=8 * 2**20),
    )(*(pltpu.with_memory_space_constraint(x, pltpu.HBM) for x in (amplitudes, integrals, slot_cd, slot_ab)))


def accumulate(slot_operands, slot_tiles, ab_list):
    row_count = slot_operands.shape[0]
    widths = slot_tiles.shape[-1]
    products = jnp.einsum(
        "rsc,scd->rsd", slot_operands, slot_tiles, preferred_element_type=jnp.float32
    )
    select = (ab_list[:, None] == jnp.arange(NT_DEV, dtype=jnp.int32)[None, :]).astype(jnp.float32)
    summed = jnp.einsum("rsd,sa->rad", products, select)
    return summed.reshape(row_count, NT_DEV * widths)


def by_slabs(amplitudes, integrals, slot_cd, slot_ab):
    groups = lax.axis_size("grp")
    own_index = lax.axis_index("grp")
    widths = integrals.shape[-1]
    pairs = amplitudes.shape[1] * lax.axis_size("tile")
    cd_table = slot_cd[0].reshape(groups, groups)
    ab_table = slot_ab[0].reshape(groups, groups)
    own_tiles = integrals[0]
    moved_tiles = lax.all_to_all(own_tiles, "grp", split_axis=0, concat_axis=0, tiled=True)
    cd_list = lax.dynamic_index_in_dim(cd_table, own_index, 1, keepdims=False)
    ab_list = lax.dynamic_index_in_dim(ab_table, own_index, 1, keepdims=False)
    outputs = []
    for batch_index in range(BATCH):
        slab_block = lax.all_gather(amplitudes[batch_index], "tile", axis=0, tiled=True)
        blocks = slab_block.reshape(pairs, slab_block.shape[1] // widths, widths)
        operands = jnp.take(blocks, cd_list, axis=1)
        full_terms = accumulate(operands, moved_tiles, ab_list)
        partial_value = lax.psum_scatter(full_terms, "grp", scatter_dimension=0, tiled=True)
        outputs.append((0.5 * partial_value).astype(jnp.bfloat16))
    return jnp.stack(outputs)


def solution(mesh):
    groups, tiles = mesh.shape["grp"], mesh.shape["tile"]

    def per_device(amplitudes, integrals, slot_cd, slot_ab):
        gathered = amplitudes.size * amplitudes.dtype.itemsize * groups * tiles
        if gathered > GATHER_LIMIT or tiles != CORES * groups or tiles & (tiles - 1):
            return by_slabs(amplitudes, integrals, slot_cd, slot_ab)
        return fused(groups, tiles, amplitudes, integrals, slot_cd, slot_ab)

    return jax.shard_map(
        per_device,
        mesh=mesh,
        in_specs=(
            P(None, "tile", "grp"),
            P("tile", "grp", None, None),
            P("tile", None),
            P("tile", None),
        ),
        out_specs=P(None, "grp", "tile"),
        check_vma=False,
    )
```

```python
import functools

import jax
import jax.numpy as jnp
from jax import lax
from jax.experimental import pallas as pl
from jax.experimental.pallas import tpu as pltpu
from jax.sharding import PartitionSpec as P

MESH = pl.DeviceIdType.MESH
NT_DEV = 2
BATCH = 2
GATHER_LIMIT = 8 * 2**20
CORES = 2


def farthest_first(own, count):
    low, high = jnp.int32(0), jnp.int32(count - 1)
    order = []
    for _ in range(count - 1):
        take_low = (own - low >= high - own).astype(jnp.int32)
        order.append(take_low * low + (1 - take_low) * high)
        low, high = low + take_low, high - (1 - take_low)
    return order


def kernel(groups, places, amp_ref, int_ref, cd_ref, ab_ref, out_ref, zbuf, xbuf, pbuf, abuf, sbuf, tile_buf, acc, rs_buf,
           sums_buf, cd_smem, ab_smem, local_sem, z_send, z_recv, t_send, t_recv, p_send, p_recv, x_send, x_recv,
           a_send, a_recv, rs_send, rs_recv):
    g, t = lax.axis_index("grp"), lax.axis_index("tile")
    place, core = lax.div(t, jnp.int32(CORES)), lax.rem(t, jnp.int32(CORES))
    widths = int_ref.shape[-1]
    tiles_dev = zbuf.shape[1]
    partner = place * CORES + 1 - core
    rest = [i + (i >= place).astype(jnp.int32) for i in range(places - 1)]
    around = [where * CORES + c for where in rest for c in range(CORES)]
    order = farthest_first(g, groups)
    nearest = order[::-1]
    piece = acc.shape[1]

    barrier = pltpu.get_barrier_semaphore()
    peers = [(t, z) for z in order] + [(column, g) for column in (partner, *around)]
    for peer in peers:
        pl.semaphore_signal(barrier, inc=1, device_id=peer, device_id_type=MESH)
    amp_copies = [
        pltpu.make_async_copy(amp_ref.at[:, :, pl.ds(c * widths, widths)], zbuf.at[g, c], local_sem.at[3])
        for c in range(tiles_dev)
    ]
    cd_copy = pltpu.make_async_copy(cd_ref, cd_smem.at[t], local_sem.at[0])
    ab_copy = pltpu.make_async_copy(ab_ref, ab_smem, local_sem.at[1])
    int_copy = pltpu.make_async_copy(int_ref, tile_buf, local_sem.at[2])
    for copy in (cd_copy, *amp_copies, ab_copy, int_copy):
        copy.start()
    pl.semaphore_wait(barrier, len(peers))

    def remote(src, dst, send, recv, peer):
        return pltpu.make_async_remote_copy(
            src_ref=src, dst_ref=dst, send_sem=send, recv_sem=recv, device_id=peer, device_id_type=MESH)

    def send(*what):
        remote(*what).start()

    def arrived(dst, recv):
        remote(dst, dst, z_send, recv, (t, z_first)).wait_recv()

    def left(src, sem):
        remote(src, src, sem, t_recv, (t, z_first)).wait_send()

    z_first = order[0]
    cd_copy.wait()
    for column in around:
        send(cd_smem.at[t], cd_smem.at[t], t_send, t_recv, (column, g))
    pltpu.make_async_copy(zbuf.at[g], zbuf.at[g], local_sem.at[3]).wait()
    for z in order:
        send(zbuf.at[g], zbuf.at[g], z_send, z_recv.at[g], (t, z))
    send(zbuf.at[g], pbuf.at[t], p_send, p_recv.at[0], (partner, g))
    for column in around:
        send(zbuf.at[g], pbuf.at[t], p_send, p_recv.at[1], (column, g))
    ab_copy.wait()
    int_copy.wait()

    def load(buf, at):
        return [buf[at, c] for c in range(tiles_dev)]

    def choose(tiles, column, j):
        cd = cd_smem[column, 0, g * groups + j]
        chosen = tiles[0]
        for c in range(1, tiles_dev):
            chosen = jnp.where(cd == c, tiles[c], chosen)
        return chosen

    def term(parts, j):
        operand = jnp.concatenate([part.reshape(-1, widths) for part in parts], axis=0)
        product = jnp.dot(operand, tile_buf[0, j], preferred_element_type=jnp.float32)
        ab = ab_smem[0, g * groups + j]
        return [product * (ab == a).astype(jnp.float32) for a in range(NT_DEV)]

    def add(left, right):
        return [x + y for x, y in zip(left, right)]

    def finish(where, totals):
        for a in range(NT_DEV):
            acc[where, :, a * widths:(a + 1) * widths] = totals[a]
            rs_buf[where, :, a * widths:(a + 1) * widths] = totals[a].astype(rs_buf.dtype)

        @pl.when(where != g)
        def _():
            send(rs_buf.at[where], sums_buf.at[g], rs_send, rs_recv, (t, where))

    arrived(pbuf.at[partner], p_recv.at[0])
    own = term([choose(load(zbuf, g), t, g), choose(load(pbuf, partner), t, g)], g)
    arrived(cd_smem.at[pl.ds(0, len(around))], t_recv)
    for k, j in enumerate(nearest):
        arrived(zbuf.at[j], z_recv.at[j])
        send(zbuf.at[j], xbuf.at[k], x_send, x_recv, (partner, g))
        tiles = load(zbuf, j)
        for e, column in enumerate(around):
            sbuf[k, e] = choose(tiles, column, j)
        for e, column in enumerate(around):
            send(sbuf.at[k, e], abuf.at[k, t], a_send, a_recv.at[k], (column, g))
    arrived(xbuf, x_recv)
    for k, j in enumerate(nearest):
        own = add(own, term([choose(load(zbuf, j), t, j), choose(load(xbuf, k), t, j)], j))
    finish(place, own)

    columns = [[where * CORES + (1 - core if r else core) for r in range(CORES)] for where in rest]
    operands = []
    arrived(pbuf.at[pl.ds(0, len(around))], p_recv.at[1])
    for pair in columns:
        for column in pair:
            operands.append(choose(load(pbuf, column), t, g))
    sums = term(operands, g)

    for k, j in enumerate(nearest):
        arrived(abuf.at[k, pl.ds(0, len(around))], a_recv.at[k])
        sums = add(sums, term([abuf[k, column] for pair in columns for column in pair], j))
    for at, where in enumerate(rest):
        finish(where, [x[at * piece:(at + 1) * piece] for x in sums])

    total = acc[g]
    arrived(sums_buf.at[pl.ds(0, groups - 1)], rs_recv)
    for j in nearest:
        total = total + sums_buf[j].astype(jnp.float32)
    total = (0.5 * total).astype(out_ref.dtype)
    half = total.shape[0] // CORES
    shape = (out_ref.shape[0], out_ref.shape[1] // CORES, out_ref.shape[2])
    same, other = total[:half].reshape(shape), total[half:].reshape(shape)
    first = core == 0
    out_ref[:, :shape[1], :] = jnp.where(first, same, other)
    out_ref[:, shape[1]:, :] = jnp.where(first, other, same)
    left(cd_smem.at[pl.ds(0, len(around))], t_send)
    left(zbuf.at[pl.ds(0, groups - 1)], z_send)
    left(pbuf.at[pl.ds(0, len(around) + 1)], p_send)
    left(xbuf, x_send)
    left(sbuf, a_send)
    left(rs_buf.at[pl.ds(0, groups - 1)], rs_send)


def fused(groups, tiles, amplitudes, integrals, slot_cd, slot_ab):
    batch, pairs_dev, span = amplitudes.shape
    widths = integrals.shape[-1]
    places = tiles // CORES
    rows = pairs_dev * tiles // groups
    result = NT_DEV * widths
    tiles_dev = span // widths
    hbm = pl.BlockSpec(memory_space=pltpu.HBM)
    block = (tiles_dev, batch, pairs_dev, widths)
    piece = CORES * batch * pairs_dev
    others, around = groups - 1, CORES * (places - 1)
    dma = pltpu.SemaphoreType.DMA
    return pl.pallas_call(
        functools.partial(kernel, groups, places),
        out_shape=jax.ShapeDtypeStruct((batch, rows, result), jnp.bfloat16),
        in_specs=[hbm] * 4,
        out_specs=pl.BlockSpec(memory_space=pltpu.VMEM),
        scratch_shapes=[
            pltpu.VMEM((groups, *block), jnp.bfloat16),
            pltpu.VMEM((others, *block), jnp.bfloat16),
            pltpu.VMEM((tiles, *block), jnp.bfloat16),
            pltpu.VMEM((others, tiles, batch, pairs_dev, widths), jnp.bfloat16),
            pltpu.VMEM((others, around, batch, pairs_dev, widths), jnp.bfloat16),
            pltpu.VMEM(integrals.shape, jnp.bfloat16),
            pltpu.VMEM((places, piece, result), jnp.float32),
            pltpu.VMEM((places, piece, result), jnp.bfloat16),
            pltpu.VMEM((groups, piece, result), jnp.bfloat16),
            pltpu.SMEM((tiles, *slot_cd.shape), jnp.int32),
            pltpu.SMEM(slot_ab.shape, jnp.int32),
            dma((4,)),
            dma,
            dma((groups,)),
            dma,
            dma,
            dma,
            dma((2,)),
            dma,
            dma,
            dma,
            dma((others,)),
            dma,
            dma,
        ],
        compiler_params=pltpu.CompilerParams(collective_id=0, has_side_effects=True, vmem_limit_bytes=8 * 2**20),
    )(*(pltpu.with_memory_space_constraint(x, pltpu.HBM) for x in (amplitudes, integrals, slot_cd, slot_ab)))


def accumulate(slot_operands, slot_tiles, ab_list):
    row_count = slot_operands.shape[0]
    widths = slot_tiles.shape[-1]
    products = jnp.einsum(
        "rsc,scd->rsd", slot_operands, slot_tiles, preferred_element_type=jnp.float32
    )
    select = (ab_list[:, None] == jnp.arange(NT_DEV, dtype=jnp.int32)[None, :]).astype(jnp.float32)
    summed = jnp.einsum("rsd,sa->rad", products, select)
    return summed.reshape(row_count, NT_DEV * widths)


def by_slabs(amplitudes, integrals, slot_cd, slot_ab):
    groups = lax.axis_size("grp")
    own_index = lax.axis_index("grp")
    widths = integrals.shape[-1]
    pairs = amplitudes.shape[1] * lax.axis_size("tile")
    cd_table = slot_cd[0].reshape(groups, groups)
    ab_table = slot_ab[0].reshape(groups, groups)
    own_tiles = integrals[0]
    moved_tiles = lax.all_to_all(own_tiles, "grp", split_axis=0, concat_axis=0, tiled=True)
    cd_list = lax.dynamic_index_in_dim(cd_table, own_index, 1, keepdims=False)
    ab_list = lax.dynamic_index_in_dim(ab_table, own_index, 1, keepdims=False)
    outputs = []
    for batch_index in range(BATCH):
        slab_block = lax.all_gather(amplitudes[batch_index], "tile", axis=0, tiled=True)
        blocks = slab_block.reshape(pairs, slab_block.shape[1] // widths, widths)
        operands = jnp.take(blocks, cd_list, axis=1)
        full_terms = accumulate(operands, moved_tiles, ab_list)
        partial_value = lax.psum_scatter(full_terms, "grp", scatter_dimension=0, tiled=True)
        outputs.append((0.5 * partial_value).astype(jnp.bfloat16))
    return jnp.stack(outputs)


def solution(mesh):
    groups, tiles = mesh.shape["grp"], mesh.shape["tile"]

    def per_device(amplitudes, integrals, slot_cd, slot_ab):
        gathered = amplitudes.size * amplitudes.dtype.itemsize * groups * tiles
        if gathered > GATHER_LIMIT or tiles != CORES * groups or tiles & (tiles - 1):
            return by_slabs(amplitudes, integrals, slot_cd, slot_ab)
        return fused(groups, tiles, amplitudes, integrals, slot_cd, slot_ab)

    return jax.shard_map(
        per_device,
        mesh=mesh,
        in_specs=(
            P(None, "tile", "grp"),
            P("tile", "grp", None, None),
            P("tile", None),
            P("tile", None),
        ),
        out_specs=P(None, "grp", "tile"),
        check_vma=False,
    )
```

```python
import functools

import jax
import jax.numpy as jnp
from jax import lax
from jax.experimental import pallas as pl
from jax.experimental.pallas import tpu as pltpu
from jax.sharding import PartitionSpec as P

MESH = pl.DeviceIdType.MESH
NT_DEV = 2
BATCH = 2
GATHER_LIMIT = 8 * 2**20
CORES = 2


def farthest_first(own, count):
    low, high = jnp.int32(0), jnp.int32(count - 1)
    order = []
    for _ in range(count - 1):
        take_low = (own - low >= high - own).astype(jnp.int32)
        order.append(take_low * low + (1 - take_low) * high)
        low, high = low + take_low, high - (1 - take_low)
    return order


def flip(index, mask):
    bit = 1
    while bit <= mask:
        if mask & bit:
            index = index + bit * (1 - 2 * lax.rem(lax.div(index, jnp.int32(bit)), jnp.int32(2)))
        bit *= 2
    return index


def kernel(groups, places, amp_ref, int_ref, cd_ref, ab_ref, out_ref, zbuf, xbuf, pbuf, abuf, sbuf, tile_buf, acc, rs_buf,
           sums_buf, cd_smem, ab_smem, local_sem, z_send, z_recv, t_send, t_recv, p_send, p_recv, x_send, x_recv,
           a_send, a_recv, rs_send, rs_recv):
    g, t = lax.axis_index("grp"), lax.axis_index("tile")
    place, core = lax.div(t, jnp.int32(CORES)), lax.rem(t, jnp.int32(CORES))
    widths = int_ref.shape[-1]
    _, batch, tiles_dev, pairs_dev, _ = zbuf.shape
    piece = CORES * pairs_dev
    partner = place * CORES + 1 - core
    rest = [flip(place, q) for q in (*range(places // 2, places), *range(1, places // 2))]
    around = [where * CORES + c for where in rest for c in range(CORES)]
    columns = [[where * CORES + (1 - core if r else core) for r in range(CORES)] for where in rest]
    order = farthest_first(g, groups)
    nearest = order[::-1]

    barrier = pltpu.get_barrier_semaphore()
    peers = [(t, z) for z in order] + [(column, g) for column in (partner, *around)]
    for peer in peers:
        pl.semaphore_signal(barrier, inc=1, device_id=peer, device_id_type=MESH)
    cd_copy = pltpu.make_async_copy(cd_ref, cd_smem.at[t], local_sem.at[0])
    ab_copy = pltpu.make_async_copy(ab_ref, ab_smem, local_sem.at[1])
    int_copy = pltpu.make_async_copy(int_ref, tile_buf, local_sem.at[2])
    cd_copy.start()
    for h in range(batch):
        for c in range(tiles_dev):
            pltpu.make_async_copy(amp_ref.at[h, :, pl.ds(c * widths, widths)], zbuf.at[g, h, c], local_sem.at[3]).start()
    ab_copy.start()
    int_copy.start()
    pl.semaphore_wait(barrier, len(peers))

    def send(src, dst, sent, recv, peer):
        pltpu.make_async_remote_copy(
            src_ref=src, dst_ref=dst, send_sem=sent, recv_sem=recv, device_id=peer, device_id_type=MESH).start()

    def arrived(dst, recv):
        pltpu.make_async_remote_copy(
            src_ref=dst, dst_ref=dst, send_sem=z_send, recv_sem=recv, device_id=peers[0], device_id_type=MESH).wait_recv()

    def left(src, sent):
        pltpu.make_async_remote_copy(
            src_ref=src, dst_ref=src, send_sem=sent, recv_sem=t_recv, device_id=peers[0], device_id_type=MESH).wait_send()

    cd_copy.wait()
    for column in around:
        send(cd_smem.at[t], cd_smem.at[t], t_send, t_recv, (column, g))
    pltpu.make_async_copy(zbuf.at[g], zbuf.at[g], local_sem.at[3]).wait()
    for h in range(batch):
        for z in order[::-1]:
            send(zbuf.at[g, h], zbuf.at[g, h], z_send, z_recv.at[g, h], (t, z))
    send(zbuf.at[g], pbuf.at[t], p_send, p_recv.at[0], (partner, g))
    for column in around:
        send(zbuf.at[g], pbuf.at[t], p_send, p_recv.at[1], (column, g))
    ab_copy.wait()
    int_copy.wait()

    def load(*at):
        buf, *at = at
        return [buf[(*at, c)] for c in range(tiles_dev)]

    def choose(tiles, column, j):
        cd = cd_smem[column, 0, g * groups + j]
        chosen = tiles[0]
        for c in range(1, tiles_dev):
            chosen = jnp.where(cd == c, tiles[c], chosen)
        return chosen

    def term(parts, j):
        operand = jnp.concatenate(parts, axis=0)
        product = jnp.dot(operand, tile_buf[0, j], preferred_element_type=jnp.float32)
        ab = ab_smem[0, g * groups + j]
        return [product * (ab == a).astype(jnp.float32) for a in range(NT_DEV)]

    def add(left, right):
        return [x + y for x, y in zip(left, right)]

    def finish(h, where, totals):
        for a in range(NT_DEV):
            acc[h, where, :, a * widths:(a + 1) * widths] = totals[a]
            rs_buf[h, where, :, a * widths:(a + 1) * widths] = totals[a].astype(rs_buf.dtype)

        @pl.when(where != g)
        def _():
            send(rs_buf.at[h, where], sums_buf.at[h, g], rs_send, rs_recv.at[h], (t, where))

    halves = range(batch)
    arrived(pbuf.at[partner], p_recv.at[0])
    own = [part for h in halves for part in (choose(load(zbuf, g, h), t, g), choose(load(pbuf, partner, h), t, g))]
    own = term(own, g)
    arrived(cd_smem.at[pl.ds(0, len(around))], t_recv)
    for h in halves:
        for k, j in enumerate(nearest):
            arrived(zbuf.at[j, h], z_recv.at[j, h])
            send(zbuf.at[j, h], xbuf.at[k, h], x_send, x_recv, (partner, g))
            tiles = load(zbuf, j, h)
            for e, column in enumerate(around):
                sbuf[h, k, e] = choose(tiles, column, j)
            for e, column in enumerate(around):
                send(sbuf.at[h, k, e], abuf.at[h, k, t], a_send, a_recv.at[h, k], (column, g))
    arrived(xbuf, x_recv)
    for k, j in enumerate(nearest):
        parts = [part for h in halves for part in (choose(load(zbuf, j, h), t, j), choose(load(xbuf, k, h), t, j))]
        own = add(own, term(parts, j))
    for h in halves:
        finish(h, place, [x[h * piece:(h + 1) * piece] for x in own])

    arrived(pbuf.at[pl.ds(0, len(around))], p_recv.at[1])
    parts = [choose(load(pbuf, column, h), t, g) for h in halves for pair in columns for column in pair]
    base = term(parts, g)
    rows = piece * len(rest)
    for h in halves:
        sums = [x[h * rows:(h + 1) * rows] for x in base]
        for k, j in enumerate(nearest):
            arrived(abuf.at[h, k, pl.ds(0, len(around))], a_recv.at[h, k])
            sums = add(sums, term([abuf[h, k, column] for pair in columns for column in pair], j))
        for at, where in enumerate(rest):
            finish(h, where, [x[at * piece:(at + 1) * piece] for x in sums])

    first = core == 0
    for h in halves:
        total = acc[h, g]
        arrived(sums_buf.at[h, pl.ds(0, groups - 1)], rs_recv.at[h])
        for j in nearest:
            total = total + sums_buf[h, j].astype(jnp.float32)
        total = (0.5 * total).astype(out_ref.dtype)
        same, other = total[:pairs_dev], total[pairs_dev:]
        out_ref[h, :pairs_dev, :] = jnp.where(first, same, other)
        out_ref[h, pairs_dev:, :] = jnp.where(first, other, same)
    left(cd_smem.at[pl.ds(0, len(around))], t_send)
    left(zbuf.at[pl.ds(0, groups - 1)], z_send)
    left(pbuf.at[pl.ds(0, len(around) + 1)], p_send)
    left(xbuf, x_send)
    left(sbuf, a_send)
    left(rs_buf.at[:, pl.ds(0, groups - 1)], rs_send)


def fused(groups, tiles, amplitudes, integrals, slot_cd, slot_ab):
    batch, pairs_dev, span = amplitudes.shape
    widths = integrals.shape[-1]
    places = tiles // CORES
    rows = pairs_dev * tiles // groups
    result = NT_DEV * widths
    tiles_dev = span // widths
    hbm = pl.BlockSpec(memory_space=pltpu.HBM)
    block = (batch, tiles_dev, pairs_dev, widths)
    piece = CORES * pairs_dev
    others, around = groups - 1, CORES * (places - 1)
    dma = pltpu.SemaphoreType.DMA
    return pl.pallas_call(
        functools.partial(kernel, groups, places),
        out_shape=jax.ShapeDtypeStruct((batch, rows, result), jnp.bfloat16),
        in_specs=[hbm] * 4,
        out_specs=pl.BlockSpec(memory_space=pltpu.VMEM),
        scratch_shapes=[
            pltpu.VMEM((groups, *block), jnp.bfloat16),
            pltpu.VMEM((others, *block), jnp.bfloat16),
            pltpu.VMEM((tiles, *block), jnp.bfloat16),
            pltpu.VMEM((batch, others, tiles, pairs_dev, widths), jnp.bfloat16),
            pltpu.VMEM((batch, others, around, pairs_dev, widths), jnp.bfloat16),
            pltpu.VMEM(integrals.shape, jnp.bfloat16),
            pltpu.VMEM((batch, places, piece, result), jnp.float32),
            pltpu.VMEM((batch, places, piece, result), jnp.bfloat16),
            pltpu.VMEM((batch, groups, piece, result), jnp.bfloat16),
            pltpu.SMEM((tiles, *slot_cd.shape), jnp.int32),
            pltpu.SMEM(slot_ab.shape, jnp.int32),
            dma((4,)),
            dma,
            dma((groups, batch)),
            dma,
            dma,
            dma,
            dma((2,)),
            dma,
            dma,
            dma,
            dma((batch, others)),
            dma,
            dma((batch,)),
        ],
        compiler_params=pltpu.CompilerParams(collective_id=0, has_side_effects=True, vmem_limit_bytes=8 * 2**20),
    )(*(pltpu.with_memory_space_constraint(x, pltpu.HBM) for x in (amplitudes, integrals, slot_cd, slot_ab)))


def accumulate(slot_operands, slot_tiles, ab_list):
    row_count = slot_operands.shape[0]
    widths = slot_tiles.shape[-1]
    products = jnp.einsum(
        "rsc,scd->rsd", slot_operands, slot_tiles, preferred_element_type=jnp.float32
    )
    select = (ab_list[:, None] == jnp.arange(NT_DEV, dtype=jnp.int32)[None, :]).astype(jnp.float32)
    summed = jnp.einsum("rsd,sa->rad", products, select)
    return summed.reshape(row_count, NT_DEV * widths)


def by_slabs(amplitudes, integrals, slot_cd, slot_ab):
    groups = lax.axis_size("grp")
    own_index = lax.axis_index("grp")
    widths = integrals.shape[-1]
    pairs = amplitudes.shape[1] * lax.axis_size("tile")
    cd_table = slot_cd[0].reshape(groups, groups)
    ab_table = slot_ab[0].reshape(groups, groups)
    own_tiles = integrals[0]
    moved_tiles = lax.all_to_all(own_tiles, "grp", split_axis=0, concat_axis=0, tiled=True)
    cd_list = lax.dynamic_index_in_dim(cd_table, own_index, 1, keepdims=False)
    ab_list = lax.dynamic_index_in_dim(ab_table, own_index, 1, keepdims=False)
    outputs = []
    for batch_index in range(BATCH):
        slab_block = lax.all_gather(amplitudes[batch_index], "tile", axis=0, tiled=True)
        blocks = slab_block.reshape(pairs, slab_block.shape[1] // widths, widths)
        operands = jnp.take(blocks, cd_list, axis=1)
        full_terms = accumulate(operands, moved_tiles, ab_list)
        partial_value = lax.psum_scatter(full_terms, "grp", scatter_dimension=0, tiled=True)
        outputs.append((0.5 * partial_value).astype(jnp.bfloat16))
    return jnp.stack(outputs)


def solution(mesh):
    groups, tiles = mesh.shape["grp"], mesh.shape["tile"]

    def per_device(amplitudes, integrals, slot_cd, slot_ab):
        gathered = amplitudes.size * amplitudes.dtype.itemsize * groups * tiles
        if gathered > GATHER_LIMIT or tiles != CORES * groups or tiles & (tiles - 1):
            return by_slabs(amplitudes, integrals, slot_cd, slot_ab)
        return fused(groups, tiles, amplitudes, integrals, slot_cd, slot_ab)

    return jax.shard_map(
        per_device,
        mesh=mesh,
        in_specs=(
            P(None, "tile", "grp"),
            P("tile", "grp", None, None),
            P("tile", None),
            P("tile", None),
        ),
        out_specs=P(None, "grp", "tile"),
        check_vma=False,
    )
```

```python
import functools

import jax
import jax.numpy as jnp
from jax import lax
from jax.experimental import pallas as pl
from jax.experimental.pallas import tpu as pltpu
from jax.sharding import PartitionSpec as P

MESH = pl.DeviceIdType.MESH
NT_DEV = 2
BATCH = 2
GATHER_LIMIT = 8 * 2**20
CORES = 2


def farthest_first(own, count):
    low, high = jnp.int32(0), jnp.int32(count - 1)
    order = []
    for _ in range(count - 1):
        take_low = (own - low >= high - own).astype(jnp.int32)
        order.append(take_low * low + (1 - take_low) * high)
        low, high = low + take_low, high - (1 - take_low)
    return order


def flip(index, mask):
    bit = 1
    while bit <= mask:
        if mask & bit:
            index = index + bit * (1 - 2 * lax.rem(lax.div(index, jnp.int32(bit)), jnp.int32(2)))
        bit *= 2
    return index


def kernel(groups, places, amp_ref, int_ref, cd_ref, ab_ref, out_ref, zbuf, xbuf, pbuf, abuf, sbuf, tile_buf, acc, rs_buf,
           sums_buf, cd_smem, ab_smem, local_sem, z_send, z_recv, t_send, t_recv, p_send, p_recv, x_send, x_recv,
           a_send, a_recv, rs_send, rs_recv):
    g, t = lax.axis_index("grp"), lax.axis_index("tile")
    place, core = lax.div(t, jnp.int32(CORES)), lax.rem(t, jnp.int32(CORES))
    widths = int_ref.shape[-1]
    _, batch, tiles_dev, pairs_dev, _ = zbuf.shape
    piece = CORES * pairs_dev
    partner = place * CORES + 1 - core
    rest = [flip(place, q) for q in (*range(places // 2, places), *range(1, places // 2))]
    around = [where * CORES + c for where in rest for c in range(CORES)]
    rising = [i + (i >= place).astype(jnp.int32) for i in range(places - 1)]
    columns = [[where * CORES + (1 - core if r else core) for r in range(CORES)] for where in rising]
    order = farthest_first(g, groups)
    nearest = order[::-1]

    barrier = pltpu.get_barrier_semaphore()
    peers = [(t, z) for z in order] + [(column, g) for column in (partner, *around)]
    for peer in peers:
        pl.semaphore_signal(barrier, inc=1, device_id=peer, device_id_type=MESH)
    cd_copy = pltpu.make_async_copy(cd_ref, cd_smem.at[t], local_sem.at[0])
    ab_copy = pltpu.make_async_copy(ab_ref, ab_smem, local_sem.at[1])
    int_copy = pltpu.make_async_copy(int_ref, tile_buf, local_sem.at[2])
    cd_copy.start()
    for h in range(batch):
        for c in range(tiles_dev):
            pltpu.make_async_copy(amp_ref.at[h, :, pl.ds(c * widths, widths)], zbuf.at[g, h, c], local_sem.at[3]).start()
    ab_copy.start()
    int_copy.start()
    pl.semaphore_wait(barrier, len(peers))

    def send(src, dst, sent, recv, peer):
        pltpu.make_async_remote_copy(
            src_ref=src, dst_ref=dst, send_sem=sent, recv_sem=recv, device_id=peer, device_id_type=MESH).start()

    def arrived(dst, recv):
        pltpu.make_async_remote_copy(
            src_ref=dst, dst_ref=dst, send_sem=z_send, recv_sem=recv, device_id=peers[0], device_id_type=MESH).wait_recv()

    def left(src, sent):
        pltpu.make_async_remote_copy(
            src_ref=src, dst_ref=src, send_sem=sent, recv_sem=t_recv, device_id=peers[0], device_id_type=MESH).wait_send()

    cd_copy.wait()
    for column in around:
        send(cd_smem.at[t], cd_smem.at[t], t_send, t_recv, (column, g))
    pltpu.make_async_copy(zbuf.at[g], zbuf.at[g], local_sem.at[3]).wait()
    for h in range(batch):
        for z in order[::-1]:
            send(zbuf.at[g, h], zbuf.at[g, h], z_send, z_recv.at[g, h], (t, z))
    send(zbuf.at[g], pbuf.at[t], p_send, p_recv.at[0], (partner, g))
    for column in around:
        send(zbuf.at[g], pbuf.at[t], p_send, p_recv.at[1], (column, g))
    ab_copy.wait()
    int_copy.wait()

    def load(*at):
        buf, *at = at
        return [buf[(*at, c)] for c in range(tiles_dev)]

    def choose(tiles, column, j):
        cd = cd_smem[column, 0, g * groups + j]
        chosen = tiles[0]
        for c in range(1, tiles_dev):
            chosen = jnp.where(cd == c, tiles[c], chosen)
        return chosen

    def term(parts, j):
        operand = jnp.concatenate(parts, axis=0)
        product = jnp.dot(operand, tile_buf[0, j], preferred_element_type=jnp.float32)
        ab = ab_smem[0, g * groups + j]
        return [product * (ab == a).astype(jnp.float32) for a in range(NT_DEV)]

    def add(left, right):
        return [x + y for x, y in zip(left, right)]

    def finish(h, where, totals):
        for a in range(NT_DEV):
            acc[h, where, :, a * widths:(a + 1) * widths] = totals[a]
            rs_buf[h, where, :, a * widths:(a + 1) * widths] = totals[a].astype(rs_buf.dtype)

        @pl.when(where != g)
        def _():
            send(rs_buf.at[h, where], sums_buf.at[h, g], rs_send, rs_recv.at[h], (t, where))

    halves = range(batch)
    arrived(pbuf.at[partner], p_recv.at[0])
    own = [part for h in halves for part in (choose(load(zbuf, g, h), t, g), choose(load(pbuf, partner, h), t, g))]
    own = term(own, g)
    arrived(cd_smem.at[pl.ds(0, len(around))], t_recv)
    for h in halves:
        for k, j in enumerate(nearest):
            arrived(zbuf.at[j, h], z_recv.at[j, h])
            send(zbuf.at[j, h], xbuf.at[k, h], x_send, x_recv, (partner, g))
            tiles = load(zbuf, j, h)
            for e, column in enumerate(around):
                sbuf[h, k, e] = choose(tiles, column, j)
            for e, column in enumerate(around):
                send(sbuf.at[h, k, e], abuf.at[h, k, t], a_send, a_recv.at[h, place], (column, g))
    arrived(xbuf, x_recv)
    for k, j in enumerate(nearest):
        parts = [part for h in halves for part in (choose(load(zbuf, j, h), t, j), choose(load(xbuf, k, h), t, j))]
        own = add(own, term(parts, j))
    for h in halves:
        finish(h, place, [x[h * piece:(h + 1) * piece] for x in own])

    arrived(pbuf.at[pl.ds(0, len(around))], p_recv.at[1])
    parts = [choose(load(pbuf, column, h), t, g) for h in halves for pair in columns for column in pair]
    base = term(parts, g)
    for h, at in ((h, at) for h in halves for at in range(places - 1)):
        where, pair = rising[at], columns[at]
        start = (h * len(rising) + at) * piece
        sums = [x[start:start + piece] for x in base]
        arrived(abuf.at[h, :, pl.ds(0, CORES)], a_recv.at[h, where])
        for k, j in enumerate(nearest):
            sums = add(sums, term([abuf[h, k, column] for column in pair], j))
        finish(h, where, sums)

    first = core == 0
    for h in halves:
        total = acc[h, g]
        arrived(sums_buf.at[h, pl.ds(0, groups - 1)], rs_recv.at[h])
        for j in nearest:
            total = total + sums_buf[h, j].astype(jnp.float32)
        total = (0.5 * total).astype(out_ref.dtype)
        same, other = total[:pairs_dev], total[pairs_dev:]
        out_ref[h, :pairs_dev, :] = jnp.where(first, same, other)
        out_ref[h, pairs_dev:, :] = jnp.where(first, other, same)
    left(cd_smem.at[pl.ds(0, len(around))], t_send)
    left(zbuf.at[pl.ds(0, groups - 1)], z_send)
    left(pbuf.at[pl.ds(0, len(around) + 1)], p_send)
    left(xbuf, x_send)
    left(sbuf, a_send)
    left(rs_buf.at[:, pl.ds(0, groups - 1)], rs_send)


def fused(groups, tiles, amplitudes, integrals, slot_cd, slot_ab):
    batch, pairs_dev, span = amplitudes.shape
    widths = integrals.shape[-1]
    places = tiles // CORES
    rows = pairs_dev * tiles // groups
    result = NT_DEV * widths
    tiles_dev = span // widths
    hbm = pl.BlockSpec(memory_space=pltpu.HBM)
    block = (batch, tiles_dev, pairs_dev, widths)
    piece = CORES * pairs_dev
    others, around = groups - 1, CORES * (places - 1)
    dma = pltpu.SemaphoreType.DMA
    return pl.pallas_call(
        functools.partial(kernel, groups, places),
        out_shape=jax.ShapeDtypeStruct((batch, rows, result), jnp.bfloat16),
        in_specs=[hbm] * 4,
        out_specs=pl.BlockSpec(memory_space=pltpu.VMEM),
        scratch_shapes=[
            pltpu.VMEM((groups, *block), jnp.bfloat16),
            pltpu.VMEM((others, *block), jnp.bfloat16),
            pltpu.VMEM((tiles, *block), jnp.bfloat16),
            pltpu.VMEM((batch, others, tiles, pairs_dev, widths), jnp.bfloat16),
            pltpu.VMEM((batch, others, around, pairs_dev, widths), jnp.bfloat16),
            pltpu.VMEM(integrals.shape, jnp.bfloat16),
            pltpu.VMEM((batch, places, piece, result), jnp.float32),
            pltpu.VMEM((batch, places, piece, result), jnp.bfloat16),
            pltpu.VMEM((batch, groups, piece, result), jnp.bfloat16),
            pltpu.SMEM((tiles, *slot_cd.shape), jnp.int32),
            pltpu.SMEM(slot_ab.shape, jnp.int32),
            dma((4,)),
            dma,
            dma((groups, batch)),
            dma,
            dma,
            dma,
            dma((2,)),
            dma,
            dma,
            dma,
            dma((batch, places)),
            dma,
            dma((batch,)),
        ],
        compiler_params=pltpu.CompilerParams(collective_id=0, has_side_effects=True, vmem_limit_bytes=8 * 2**20),
    )(*(pltpu.with_memory_space_constraint(x, pltpu.HBM) for x in (amplitudes, integrals, slot_cd, slot_ab)))


def accumulate(slot_operands, slot_tiles, ab_list):
    row_count = slot_operands.shape[0]
    widths = slot_tiles.shape[-1]
    products = jnp.einsum(
        "rsc,scd->rsd", slot_operands, slot_tiles, preferred_element_type=jnp.float32
    )
    select = (ab_list[:, None] == jnp.arange(NT_DEV, dtype=jnp.int32)[None, :]).astype(jnp.float32)
    summed = jnp.einsum("rsd,sa->rad", products, select)
    return summed.reshape(row_count, NT_DEV * widths)


def by_slabs(amplitudes, integrals, slot_cd, slot_ab):
    groups = lax.axis_size("grp")
    own_index = lax.axis_index("grp")
    widths = integrals.shape[-1]
    pairs = amplitudes.shape[1] * lax.axis_size("tile")
    cd_table = slot_cd[0].reshape(groups, groups)
    ab_table = slot_ab[0].reshape(groups, groups)
    own_tiles = integrals[0]
    moved_tiles = lax.all_to_all(own_tiles, "grp", split_axis=0, concat_axis=0, tiled=True)
    cd_list = lax.dynamic_index_in_dim(cd_table, own_index, 1, keepdims=False)
    ab_list = lax.dynamic_index_in_dim(ab_table, own_index, 1, keepdims=False)
    outputs = []
    for batch_index in range(BATCH):
        slab_block = lax.all_gather(amplitudes[batch_index], "tile", axis=0, tiled=True)
        blocks = slab_block.reshape(pairs, slab_block.shape[1] // widths, widths)
        operands = jnp.take(blocks, cd_list, axis=1)
        full_terms = accumulate(operands, moved_tiles, ab_list)
        partial_value = lax.psum_scatter(full_terms, "grp", scatter_dimension=0, tiled=True)
        outputs.append((0.5 * partial_value).astype(jnp.bfloat16))
    return jnp.stack(outputs)


def solution(mesh):
    groups, tiles = mesh.shape["grp"], mesh.shape["tile"]

    def per_device(amplitudes, integrals, slot_cd, slot_ab):
        gathered = amplitudes.size * amplitudes.dtype.itemsize * groups * tiles
        if gathered > GATHER_LIMIT or tiles != CORES * groups or tiles & (tiles - 1):
            return by_slabs(amplitudes, integrals, slot_cd, slot_ab)
        return fused(groups, tiles, amplitudes, integrals, slot_cd, slot_ab)

    return jax.shard_map(
        per_device,
        mesh=mesh,
        in_specs=(
            P(None, "tile", "grp"),
            P("tile", "grp", None, None),
            P("tile", None),
            P("tile", None),
        ),
        out_specs=P(None, "grp", "tile"),
        check_vma=False,
    )
```

```python
import functools

import jax
import jax.numpy as jnp
from jax import lax
from jax.experimental import pallas as pl
from jax.experimental.pallas import tpu as pltpu
from jax.sharding import PartitionSpec as P

MESH = pl.DeviceIdType.MESH
NT_DEV = 2
BATCH = 2
GATHER_LIMIT = 8 * 2**20
CORES = 2


def farthest_first(own, count):
    low, high = jnp.int32(0), jnp.int32(count - 1)
    order = []
    for _ in range(count - 1):
        take_low = (own - low >= high - own).astype(jnp.int32)
        order.append(take_low * low + (1 - take_low) * high)
        low, high = low + take_low, high - (1 - take_low)
    return order


def without(index, absent):
    return index - (index > absent).astype(jnp.int32)


def kernel(groups, places, amp_ref, int_ref, cd_ref, ab_ref, out_ref, zbuf, xbuf, pbuf, abuf, sbuf, tile_buf, acc, rs_buf,
           sums_buf, all_sent, tables, local_sem, sent, z_recv, t_send, t_recv, p_recv, x_recv, a_recv, rs_recv):
    g, t = lax.axis_index("grp"), lax.axis_index("tile")
    place, core = lax.div(t, jnp.int32(CORES)), lax.rem(t, jnp.int32(CORES))
    widths = int_ref.shape[-1]
    _, batch, tiles_dev, pairs_dev, _ = zbuf.shape
    piece = CORES * pairs_dev
    partner = place * CORES + 1 - core
    rest = [i + (i >= place).astype(jnp.int32) for i in range(places - 1)]
    around = [where * CORES + c for where in rest for c in range(CORES)]
    rising = [i + (i >= place).astype(jnp.int32) for i in range(places - 1)]
    columns = [[where * CORES + (1 - core if r else core) for r in range(CORES)] for where in rising]
    order = farthest_first(g, groups)
    nearest = order[::-1]

    barrier = pltpu.get_barrier_semaphore()
    peers = [(t, z) for z in order] + [(column, g) for column in (partner, *around)]
    for peer in peers:
        pl.semaphore_signal(barrier, inc=1, device_id=peer, device_id_type=MESH)
    near = places * CORES
    cd_copy = pltpu.make_async_copy(cd_ref, tables.at[t], local_sem.at[0])
    ab_copy = pltpu.make_async_copy(ab_ref, tables.at[near], local_sem.at[0])
    int_copy = pltpu.make_async_copy(int_ref, tile_buf, local_sem.at[1])
    cd_copy.start()
    ab_copy.start()
    for h in range(batch):
        for c in range(tiles_dev):
            pltpu.make_async_copy(amp_ref.at[h, :, pl.ds(c * widths, widths)], zbuf.at[g, h, c], local_sem.at[2]).start()
    int_copy.start()
    pl.semaphore_wait(barrier, len(peers))

    def send(src, dst, gone, recv, peer):
        pltpu.make_async_remote_copy(
            src_ref=src, dst_ref=dst, send_sem=gone, recv_sem=recv, device_id=peer, device_id_type=MESH).start()

    def arrived(dst, recv):
        pltpu.make_async_remote_copy(
            src_ref=dst, dst_ref=dst, send_sem=sent, recv_sem=recv, device_id=peers[0], device_id_type=MESH).wait_recv()

    def left(src, gone):
        pltpu.make_async_remote_copy(
            src_ref=src, dst_ref=src, send_sem=gone, recv_sem=t_recv, device_id=peers[0], device_id_type=MESH).wait_send()

    pltpu.make_async_copy(tables.at[pl.ds(0, 2)], tables.at[pl.ds(0, 2)], local_sem.at[0]).wait()
    for column in around:
        send(tables.at[t], tables.at[t], t_send, t_recv, (column, g))
    pltpu.make_async_copy(zbuf.at[g], zbuf.at[g], local_sem.at[2]).wait()
    for h in range(batch):
        for z in order[::-1]:
            send(zbuf.at[g, h], zbuf.at[g, h], sent, z_recv.at[without(g, z), h], (t, z))
    send(zbuf.at[g], pbuf.at[t], sent, p_recv.at[0], (partner, g))
    for column in around:
        send(zbuf.at[g], pbuf.at[t], sent, p_recv.at[1], (column, g))
    int_copy.wait()

    def load(*at):
        buf, *at = at
        return [buf[(*at, c)] for c in range(tiles_dev)]

    def choose(tiles, column, j):
        cd = tables[column, 0, g * groups + j]
        chosen = tiles[0]
        for c in range(1, tiles_dev):
            chosen = jnp.where(cd == c, tiles[c], chosen)
        return chosen

    def term(parts, j):
        operand = jnp.concatenate(parts, axis=0)
        product = jnp.dot(operand, tile_buf[0, j], preferred_element_type=jnp.float32)
        ab = tables[near, 0, g * groups + j]
        return [product * (ab == a).astype(jnp.float32) for a in range(NT_DEV)]

    def add(left, right):
        return [x + y for x, y in zip(left, right)]

    def finish(h, where, totals):
        for a in range(NT_DEV):
            acc[h, where, :, a * widths:(a + 1) * widths] = totals[a]
            rs_buf[h, where, :, a * widths:(a + 1) * widths] = totals[a].astype(rs_buf.dtype)

        @pl.when(where != g)
        def _():
            send(rs_buf.at[h, where], sums_buf.at[h, g], sent, rs_recv.at[h], (t, where))

    halves = range(batch)
    arrived(pbuf.at[partner], p_recv.at[0])
    own = [part for h in halves for part in (choose(load(zbuf, g, h), t, g), choose(load(pbuf, partner, h), t, g))]
    own = term(own, g)
    arrived(tables.at[pl.ds(0, len(around))], t_recv)
    for h in halves:
        for k, j in enumerate(nearest):
            arrived(zbuf.at[j, h], z_recv.at[without(j, g), h])
            send(zbuf.at[j, h], xbuf.at[k, h], sent, x_recv, (partner, g))
            tiles = load(zbuf, j, h)
            for e, column in enumerate(around):
                sbuf[h, k, e] = choose(tiles, column, j)
            for e, column in enumerate(around):
                send(sbuf.at[h, k, e], abuf.at[h, k, t], sent, a_recv.at[h, without(place, rest[e // CORES])], (column, g))
    arrived(xbuf, x_recv)
    for k, j in enumerate(nearest):
        parts = [part for h in halves for part in (choose(load(zbuf, j, h), t, j), choose(load(xbuf, k, h), t, j))]
        own = add(own, term(parts, j))
    for h in halves:
        finish(h, place, [x[h * piece:(h + 1) * piece] for x in own])

    arrived(pbuf.at[pl.ds(0, len(around))], p_recv.at[1])
    parts = [choose(load(pbuf, column, h), t, g) for h in halves for pair in columns for column in pair]
    base = term(parts, g)
    def turn(h, low, high):
        start = (h * len(rising) + low) * piece
        sums = [x[start:start + (high - low) * piece] for x in base]
        for where in rising[low:high]:
            arrived(abuf.at[h, :, pl.ds(0, CORES)], a_recv.at[h, without(where, place)])
        for k, j in enumerate(nearest):
            sums = add(sums, term([abuf[h, k, column] for pair in columns[low:high] for column in pair], j))
        for at in range(low, high):
            finish(h, rising[at], [x[(at - low) * piece:(at - low + 1) * piece] for x in sums])

    @pl.when(2 * g < groups)
    def _():
        for what in ((0, 0, 2), (0, 2, 3), (1, 0, 2), (1, 2, 3)):
            turn(*what)

    @pl.when(2 * g >= groups)
    def _():
        for what in ((0, 0, 1), (1, 0, 1), (0, 1, 2), (0, 2, 3), (1, 1, 2), (1, 2, 3)):
            turn(*what)

    first = core == 0
    for h in halves:
        total = acc[h, g]
        arrived(sums_buf.at[h, pl.ds(0, groups - 1)], rs_recv.at[h])
        for j in nearest:
            total = total + sums_buf[h, j].astype(jnp.float32)
        total = (0.5 * total).astype(out_ref.dtype)
        same, other = total[:pairs_dev], total[pairs_dev:]
        out_ref[h, :pairs_dev, :] = jnp.where(first, same, other)
        out_ref[h, pairs_dev:, :] = jnp.where(first, other, same)
    left(tables.at[pl.ds(0, len(around))], t_send)
    left(all_sent, sent)


def fused(groups, tiles, amplitudes, integrals, slot_cd, slot_ab):
    batch, pairs_dev, span = amplitudes.shape
    widths = integrals.shape[-1]
    places = tiles // CORES
    rows = pairs_dev * tiles // groups
    result = NT_DEV * widths
    tiles_dev = span // widths
    hbm = pl.BlockSpec(memory_space=pltpu.HBM)
    block = (batch, tiles_dev, pairs_dev, widths)
    piece = CORES * pairs_dev
    others, around = groups - 1, CORES * (places - 1)
    dma = pltpu.SemaphoreType.DMA
    all_sent = batch * ((2 * others + tiles - 1) * tiles_dev + others * around + others * CORES * NT_DEV)
    return pl.pallas_call(
        functools.partial(kernel, groups, places),
        out_shape=jax.ShapeDtypeStruct((batch, rows, result), jnp.bfloat16),
        in_specs=[hbm] * 4,
        out_specs=pl.BlockSpec(memory_space=pltpu.VMEM),
        scratch_shapes=[
            pltpu.VMEM((groups, *block), jnp.bfloat16),
            pltpu.VMEM((others, *block), jnp.bfloat16),
            pltpu.VMEM((tiles, *block), jnp.bfloat16),
            pltpu.VMEM((batch, others, tiles, pairs_dev, widths), jnp.bfloat16),
            pltpu.VMEM((batch, others, around, pairs_dev, widths), jnp.bfloat16),
            pltpu.VMEM(integrals.shape, jnp.bfloat16),
            pltpu.VMEM((batch, places, piece, result), jnp.float32),
            pltpu.VMEM((batch, places, piece, result), jnp.bfloat16),
            pltpu.VMEM((batch, groups, piece, result), jnp.bfloat16),
            pltpu.VMEM((all_sent, pairs_dev, widths), jnp.bfloat16),
            pltpu.SMEM((tiles + 1, *slot_cd.shape), jnp.int32),
            dma((3,)),
            dma,
            dma((others, batch)),
            dma,
            dma,
            dma((2,)),
            dma,
            dma((batch, places - 1)),
            dma((batch,)),
        ],
        compiler_params=pltpu.CompilerParams(collective_id=0, has_side_effects=True, vmem_limit_bytes=8 * 2**20),
    )(*(pltpu.with_memory_space_constraint(x, pltpu.HBM) for x in (amplitudes, integrals, slot_cd, slot_ab)))


def accumulate(slot_operands, slot_tiles, ab_list):
    row_count = slot_operands.shape[0]
    widths = slot_tiles.shape[-1]
    products = jnp.einsum(
        "rsc,scd->rsd", slot_operands, slot_tiles, preferred_element_type=jnp.float32
    )
    select = (ab_list[:, None] == jnp.arange(NT_DEV, dtype=jnp.int32)[None, :]).astype(jnp.float32)
    summed = jnp.einsum("rsd,sa->rad", products, select)
    return summed.reshape(row_count, NT_DEV * widths)


def by_slabs(amplitudes, integrals, slot_cd, slot_ab):
    groups = lax.axis_size("grp")
    own_index = lax.axis_index("grp")
    widths = integrals.shape[-1]
    pairs = amplitudes.shape[1] * lax.axis_size("tile")
    cd_table = slot_cd[0].reshape(groups, groups)
    ab_table = slot_ab[0].reshape(groups, groups)
    own_tiles = integrals[0]
    moved_tiles = lax.all_to_all(own_tiles, "grp", split_axis=0, concat_axis=0, tiled=True)
    cd_list = lax.dynamic_index_in_dim(cd_table, own_index, 1, keepdims=False)
    ab_list = lax.dynamic_index_in_dim(ab_table, own_index, 1, keepdims=False)
    outputs = []
    for batch_index in range(BATCH):
        slab_block = lax.all_gather(amplitudes[batch_index], "tile", axis=0, tiled=True)
        blocks = slab_block.reshape(pairs, slab_block.shape[1] // widths, widths)
        operands = jnp.take(blocks, cd_list, axis=1)
        full_terms = accumulate(operands, moved_tiles, ab_list)
        partial_value = lax.psum_scatter(full_terms, "grp", scatter_dimension=0, tiled=True)
        outputs.append((0.5 * partial_value).astype(jnp.bfloat16))
    return jnp.stack(outputs)


def solution(mesh):
    groups, tiles = mesh.shape["grp"], mesh.shape["tile"]

    def per_device(amplitudes, integrals, slot_cd, slot_ab):
        gathered = amplitudes.size * amplitudes.dtype.itemsize * groups * tiles
        if gathered > GATHER_LIMIT or tiles != CORES * groups or tiles & (tiles - 1):
            return by_slabs(amplitudes, integrals, slot_cd, slot_ab)
        return fused(groups, tiles, amplitudes, integrals, slot_cd, slot_ab)

    return jax.shard_map(
        per_device,
        mesh=mesh,
        in_specs=(
            P(None, "tile", "grp"),
            P("tile", "grp", None, None),
            P("tile", None),
            P("tile", None),
        ),
        out_specs=P(None, "grp", "tile"),
        check_vma=False,
    )
```

```python
import functools

import jax
import jax.numpy as jnp
from jax import lax
from jax.experimental import pallas as pl
from jax.experimental.pallas import tpu as pltpu
from jax.sharding import PartitionSpec as P

MESH = pl.DeviceIdType.MESH
NT_DEV = 2
BATCH = 2
GATHER_LIMIT = 8 * 2**20
CORES = 2


def farthest_first(own, count):
    low, high = jnp.int32(0), jnp.int32(count - 1)
    order = []
    for _ in range(count - 1):
        take_low = (own - low >= high - own).astype(jnp.int32)
        order.append(take_low * low + (1 - take_low) * high)
        low, high = low + take_low, high - (1 - take_low)
    return order


def without(index, absent):
    return index - (index > absent).astype(jnp.int32)


def kernel(groups, places, amp_ref, int_ref, cd_ref, ab_ref, out_ref, zbuf, xbuf, pbuf, abuf, sbuf, tile_buf, acc, rs_buf,
           sums_buf, all_sent, tables, local_sem, sent, z_recv, t_send, t_recv, p_recv, x_recv, a_recv, rs_recv):
    g, t = lax.axis_index("grp"), lax.axis_index("tile")
    place, core = lax.div(t, jnp.int32(CORES)), lax.rem(t, jnp.int32(CORES))
    widths = int_ref.shape[-1]
    _, batch, tiles_dev, pairs_dev, _ = zbuf.shape
    piece = CORES * pairs_dev
    partner = place * CORES + 1 - core
    rest = [i + (i >= place).astype(jnp.int32) for i in range(places - 1)]
    around = [where * CORES + c for where in rest for c in range(CORES)]
    rising = [i + (i >= place).astype(jnp.int32) for i in range(places - 1)]
    columns = [[where * CORES + (1 - core if r else core) for r in range(CORES)] for where in rising]
    order = farthest_first(g, groups)
    nearest = order[::-1]
    top = (g == groups - 1).astype(jnp.int32)
    routed = [top * nearest[i] + (1 - top) * z for i, z in zip((0,2,1), nearest)]

    barrier = pltpu.get_barrier_semaphore()
    peers = [(t, z) for z in order] + [(column, g) for column in (partner, *around)]
    for peer in peers:
        pl.semaphore_signal(barrier, inc=1, device_id=peer, device_id_type=MESH)
    near = places * CORES
    cd_copy = pltpu.make_async_copy(cd_ref, tables.at[t], local_sem.at[0])
    ab_copy = pltpu.make_async_copy(ab_ref, tables.at[near], local_sem.at[0])
    int_copy = pltpu.make_async_copy(int_ref, tile_buf, local_sem.at[1])
    for h in range(batch):
        for c in range(tiles_dev):
            pltpu.make_async_copy(amp_ref.at[h, :, pl.ds(c * widths, widths)], zbuf.at[g, h, c], local_sem.at[2]).start()
    cd_copy.start()
    ab_copy.start()
    int_copy.start()
    pl.semaphore_wait(barrier, len(peers))

    def send(src, dst, gone, recv, peer):
        pltpu.make_async_remote_copy(
            src_ref=src, dst_ref=dst, send_sem=gone, recv_sem=recv, device_id=peer, device_id_type=MESH).start()

    def arrived(dst, recv):
        pltpu.make_async_remote_copy(
            src_ref=dst, dst_ref=dst, send_sem=sent, recv_sem=recv, device_id=peers[0], device_id_type=MESH).wait_recv()

    def left(src, gone):
        pltpu.make_async_remote_copy(
            src_ref=src, dst_ref=src, send_sem=gone, recv_sem=t_recv, device_id=peers[0], device_id_type=MESH).wait_send()

    pltpu.make_async_copy(zbuf.at[g], zbuf.at[g], local_sem.at[2]).wait()
    for h in range(batch):
        for z in routed:
            send(zbuf.at[g, h], zbuf.at[g, h], sent, z_recv.at[without(g, z), h], (t, z))
    pltpu.make_async_copy(tables.at[pl.ds(0, 2)], tables.at[pl.ds(0, 2)], local_sem.at[0]).wait()
    for column in around:
        send(tables.at[t], tables.at[t], t_send, t_recv, (column, g))
    send(zbuf.at[g], pbuf.at[t], sent, p_recv.at[0], (partner, g))
    for column in around:
        send(zbuf.at[g], pbuf.at[t], sent, p_recv.at[1], (column, g))
    int_copy.wait()

    def load(*at):
        buf, *at = at
        return [buf[(*at, c)] for c in range(tiles_dev)]

    def choose(tiles, column, j):
        cd = tables[column, 0, g * groups + j]
        chosen = tiles[0]
        for c in range(1, tiles_dev):
            chosen = jnp.where(cd == c, tiles[c], chosen)
        return chosen

    def term(parts, j):
        operand = jnp.concatenate(parts, axis=0)
        product = jnp.dot(operand, tile_buf[0, j], preferred_element_type=jnp.float32)
        ab = tables[near, 0, g * groups + j]
        return [product * (ab == a).astype(jnp.float32) for a in range(NT_DEV)]

    def add(left, right):
        return [x + y for x, y in zip(left, right)]

    def finish(h, where, totals):
        for a in range(NT_DEV):
            acc[h, where, :, a * widths:(a + 1) * widths] = totals[a]
            rs_buf[h, where, :, a * widths:(a + 1) * widths] = totals[a].astype(rs_buf.dtype)

        @pl.when(where != g)
        def _():
            send(rs_buf.at[h, where], sums_buf.at[h, g], sent, rs_recv.at[h], (t, where))

    halves = range(batch)
    arrived(pbuf.at[partner], p_recv.at[0])
    own = [part for h in halves for part in (choose(load(zbuf, g, h), t, g), choose(load(pbuf, partner, h), t, g))]
    own = term(own, g)
    arrived(tables.at[pl.ds(0, len(around))], t_recv)
    for h in halves:
        for k, j in enumerate(nearest):
            arrived(zbuf.at[j, h], z_recv.at[without(j, g), h])
            send(zbuf.at[j, h], xbuf.at[k, h], sent, x_recv, (partner, g))
            tiles = load(zbuf, j, h)
            for e, column in enumerate(around):
                sbuf[h, k, e] = choose(tiles, column, j)
            for e, column in enumerate(around):
                send(sbuf.at[h, k, e], abuf.at[h, k, t], sent, a_recv.at[h, without(place, rest[e // CORES])], (column, g))
    arrived(xbuf, x_recv)
    for k, j in enumerate(nearest):
        parts = [part for h in halves for part in (choose(load(zbuf, j, h), t, j), choose(load(xbuf, k, h), t, j))]
        own = add(own, term(parts, j))
    for h in halves:
        finish(h, place, [x[h * piece:(h + 1) * piece] for x in own])

    arrived(pbuf.at[pl.ds(0, len(around))], p_recv.at[1])
    parts = [choose(load(pbuf, column, h), t, g) for h in halves for pair in columns for column in pair]
    base = term(parts, g)
    def turn(h, low, high):
        start = (h * len(rising) + low) * piece
        sums = [x[start:start + (high - low) * piece] for x in base]
        for where in rising[low:high]:
            arrived(abuf.at[h, :, pl.ds(0, CORES)], a_recv.at[h, without(where, place)])
        for k, j in enumerate(nearest):
            sums = add(sums, term([abuf[h, k, column] for pair in columns[low:high] for column in pair], j))
        for at in range(low, high):
            finish(h, rising[at], [x[(at - low) * piece:(at - low + 1) * piece] for x in sums])

    @pl.when(2 * g < groups)
    def _():
        for what in ((0, 0, 2), (0, 2, 3), (1, 0, 2), (1, 2, 3)):
            turn(*what)

    @pl.when(2 * g >= groups)
    def _():
        for what in ((0, 0, 1), (1, 0, 1), (0, 1, 2), (0, 2, 3), (1, 1, 2), (1, 2, 3)):
            turn(*what)

    first = core == 0
    for h in halves:
        total = acc[h, g]
        arrived(sums_buf.at[h, pl.ds(0, groups - 1)], rs_recv.at[h])
        for j in nearest:
            total = total + sums_buf[h, j].astype(jnp.float32)
        total = (0.5 * total).astype(out_ref.dtype)
        same, other = total[:pairs_dev], total[pairs_dev:]
        out_ref[h, :pairs_dev, :] = jnp.where(first, same, other)
        out_ref[h, pairs_dev:, :] = jnp.where(first, other, same)
    left(tables.at[pl.ds(0, len(around))], t_send)
    left(all_sent, sent)


def fused(groups, tiles, amplitudes, integrals, slot_cd, slot_ab):
    batch, pairs_dev, span = amplitudes.shape
    widths = integrals.shape[-1]
    places = tiles // CORES
    rows = pairs_dev * tiles // groups
    result = NT_DEV * widths
    tiles_dev = span // widths
    hbm = pl.BlockSpec(memory_space=pltpu.HBM)
    block = (batch, tiles_dev, pairs_dev, widths)
    piece = CORES * pairs_dev
    others, around = groups - 1, CORES * (places - 1)
    dma = pltpu.SemaphoreType.DMA
    all_sent = batch * ((2 * others + tiles - 1) * tiles_dev + others * around + others * CORES * NT_DEV)
    return pl.pallas_call(
        functools.partial(kernel, groups, places),
        out_shape=jax.ShapeDtypeStruct((batch, rows, result), jnp.bfloat16),
        in_specs=[hbm] * 4,
        out_specs=pl.BlockSpec(memory_space=pltpu.VMEM),
        scratch_shapes=[
            pltpu.VMEM((groups, *block), jnp.bfloat16),
            pltpu.VMEM((others, *block), jnp.bfloat16),
            pltpu.VMEM((tiles, *block), jnp.bfloat16),
            pltpu.VMEM((batch, others, tiles, pairs_dev, widths), jnp.bfloat16),
            pltpu.VMEM((batch, others, around, pairs_dev, widths), jnp.bfloat16),
            pltpu.VMEM(integrals.shape, jnp.bfloat16),
            pltpu.VMEM((batch, places, piece, result), jnp.float32),
            pltpu.VMEM((batch, places, piece, result), jnp.bfloat16),
            pltpu.VMEM((batch, groups, piece, result), jnp.bfloat16),
            pltpu.VMEM((all_sent, pairs_dev, widths), jnp.bfloat16),
            pltpu.SMEM((tiles + 1, *slot_cd.shape), jnp.int32),
            dma((3,)),
            dma,
            dma((others, batch)),
            dma,
            dma,
            dma((2,)),
            dma,
            dma((batch, places - 1)),
            dma((batch,)),
        ],
        compiler_params=pltpu.CompilerParams(collective_id=0, has_side_effects=True, vmem_limit_bytes=8 * 2**20),
    )(*(pltpu.with_memory_space_constraint(x, pltpu.HBM) for x in (amplitudes, integrals, slot_cd, slot_ab)))


def accumulate(slot_operands, slot_tiles, ab_list):
    row_count = slot_operands.shape[0]
    widths = slot_tiles.shape[-1]
    products = jnp.einsum(
        "rsc,scd->rsd", slot_operands, slot_tiles, preferred_element_type=jnp.float32
    )
    select = (ab_list[:, None] == jnp.arange(NT_DEV, dtype=jnp.int32)[None, :]).astype(jnp.float32)
    summed = jnp.einsum("rsd,sa->rad", products, select)
    return summed.reshape(row_count, NT_DEV * widths)


def by_slabs(amplitudes, integrals, slot_cd, slot_ab):
    groups = lax.axis_size("grp")
    own_index = lax.axis_index("grp")
    widths = integrals.shape[-1]
    pairs = amplitudes.shape[1] * lax.axis_size("tile")
    cd_table = slot_cd[0].reshape(groups, groups)
    ab_table = slot_ab[0].reshape(groups, groups)
    own_tiles = integrals[0]
    moved_tiles = lax.all_to_all(own_tiles, "grp", split_axis=0, concat_axis=0, tiled=True)
    cd_list = lax.dynamic_index_in_dim(cd_table, own_index, 1, keepdims=False)
    ab_list = lax.dynamic_index_in_dim(ab_table, own_index, 1, keepdims=False)
    outputs = []
    for batch_index in range(BATCH):
        slab_block = lax.all_gather(amplitudes[batch_index], "tile", axis=0, tiled=True)
        blocks = slab_block.reshape(pairs, slab_block.shape[1] // widths, widths)
        operands = jnp.take(blocks, cd_list, axis=1)
        full_terms = accumulate(operands, moved_tiles, ab_list)
        partial_value = lax.psum_scatter(full_terms, "grp", scatter_dimension=0, tiled=True)
        outputs.append((0.5 * partial_value).astype(jnp.bfloat16))
    return jnp.stack(outputs)


def solution(mesh):
    groups, tiles = mesh.shape["grp"], mesh.shape["tile"]

    def per_device(amplitudes, integrals, slot_cd, slot_ab):
        gathered = amplitudes.size * amplitudes.dtype.itemsize * groups * tiles
        if gathered > GATHER_LIMIT or tiles != CORES * groups or tiles & (tiles - 1):
            return by_slabs(amplitudes, integrals, slot_cd, slot_ab)
        return fused(groups, tiles, amplitudes, integrals, slot_cd, slot_ab)

    return jax.shard_map(
        per_device,
        mesh=mesh,
        in_specs=(
            P(None, "tile", "grp"),
            P("tile", "grp", None, None),
            P("tile", None),
            P("tile", None),
        ),
        out_specs=P(None, "grp", "tile"),
        check_vma=False,
    )
```

```python
import functools

import jax
import jax.numpy as jnp
from jax import lax
from jax.experimental import pallas as pl
from jax.experimental.pallas import tpu as pltpu
from jax.sharding import PartitionSpec as P

MESH = pl.DeviceIdType.MESH
NT_DEV = 2
BATCH = 2
GATHER_LIMIT = 8 * 2**20
CORES = 2


def farthest_first(own, count):
    low, high = jnp.int32(0), jnp.int32(count - 1)
    order = []
    for _ in range(count - 1):
        take_low = (own - low >= high - own).astype(jnp.int32)
        order.append(take_low * low + (1 - take_low) * high)
        low, high = low + take_low, high - (1 - take_low)
    return order


def without(index, absent):
    return index - (index > absent).astype(jnp.int32)


def kernel(groups, places, amp_ref, int_ref, cd_ref, ab_ref, out_ref, zbuf, xbuf, pbuf, abuf, sbuf, tile_buf, acc, rs_buf,
           sums_buf, all_sent, tables, local_sem, sent, z_recv, t_send, t_recv, p_recv, x_recv, a_recv, rs_recv):
    g, t = lax.axis_index("grp"), lax.axis_index("tile")
    place, core = lax.div(t, jnp.int32(CORES)), lax.rem(t, jnp.int32(CORES))
    widths = int_ref.shape[-1]
    _, batch, tiles_dev, pairs_dev, _ = zbuf.shape
    piece = CORES * pairs_dev
    partner = place * CORES + 1 - core
    rest = [i + (i >= place).astype(jnp.int32) for i in range(places - 1)]
    around = [where * CORES + c for where in rest for c in range(CORES)]
    rising = [i + (i >= place).astype(jnp.int32) for i in range(places - 1)]
    columns = [[where * CORES + (1 - core if r else core) for r in range(CORES)] for where in rising]
    order = farthest_first(g, groups)
    nearest = order[::-1]
    top = (g == groups - 1).astype(jnp.int32)
    routed = [top * nearest[i] + (1 - top) * z for i, z in zip((0,2,1), nearest)]

    barrier = pltpu.get_barrier_semaphore()
    peers = [(t, z) for z in order] + [(column, g) for column in (partner, *around)]
    for peer in peers:
        pl.semaphore_signal(barrier, inc=1, device_id=peer, device_id_type=MESH)
    near = places * CORES
    cd_copy = pltpu.make_async_copy(cd_ref, tables.at[t], local_sem.at[0])
    ab_copy = pltpu.make_async_copy(ab_ref, tables.at[near], local_sem.at[0])
    int_copy = pltpu.make_async_copy(int_ref, tile_buf, local_sem.at[1])
    for h in range(batch):
        for c in range(tiles_dev):
            pltpu.make_async_copy(amp_ref.at[h, :, pl.ds(c * widths, widths)], zbuf.at[g, h, c], local_sem.at[2]).start()
    cd_copy.start()
    ab_copy.start()
    int_copy.start()
    pl.semaphore_wait(barrier, len(peers))

    def send(src, dst, gone, recv, peer):
        pltpu.make_async_remote_copy(
            src_ref=src, dst_ref=dst, send_sem=gone, recv_sem=recv, device_id=peer, device_id_type=MESH).start()

    def arrived(dst, recv):
        pltpu.make_async_remote_copy(
            src_ref=dst, dst_ref=dst, send_sem=sent, recv_sem=recv, device_id=peers[0], device_id_type=MESH).wait_recv()

    def left(src, gone):
        pltpu.make_async_remote_copy(
            src_ref=src, dst_ref=src, send_sem=gone, recv_sem=t_recv, device_id=peers[0], device_id_type=MESH).wait_send()

    pltpu.make_async_copy(zbuf.at[g], zbuf.at[g], local_sem.at[2]).wait()
    for h in range(batch):
        for z in routed:
            send(zbuf.at[g, h], zbuf.at[g, h], sent, z_recv.at[without(g, z), h], (t, z))
    pltpu.make_async_copy(tables.at[pl.ds(0, 2)], tables.at[pl.ds(0, 2)], local_sem.at[0]).wait()
    for column in around:
        send(tables.at[t], tables.at[t], t_send, t_recv, (column, g))
    send(zbuf.at[g], pbuf.at[t], sent, p_recv.at[0], (partner, g))
    for column in around:
        send(zbuf.at[g], pbuf.at[t], sent, p_recv.at[1], (column, g))
    int_copy.wait()

    def load(*at):
        buf, *at = at
        return [buf[(*at, c)] for c in range(tiles_dev)]

    def choose(tiles, column, j):
        cd = tables[column, 0, g * groups + j]
        chosen = tiles[0]
        for c in range(1, tiles_dev):
            chosen = jnp.where(cd == c, tiles[c], chosen)
        return chosen

    def term(parts, j):
        operand = jnp.concatenate(parts, axis=0)
        product = jnp.dot(operand, tile_buf[0, j], preferred_element_type=jnp.float32)
        ab = tables[near, 0, g * groups + j]
        return [product * (ab == a).astype(jnp.float32) for a in range(NT_DEV)]

    def add(left, right):
        return [x + y for x, y in zip(left, right)]

    def finish(h, where, totals):
        for a in range(NT_DEV):
            acc[h, where, :, a * widths:(a + 1) * widths] = totals[a]
            rs_buf[h, where, :, a * widths:(a + 1) * widths] = totals[a].astype(rs_buf.dtype)

        @pl.when(where != g)
        def _():
            send(rs_buf.at[h, where], sums_buf.at[h, g], sent, rs_recv.at[h], (t, where))

    halves = range(batch)
    arrived(pbuf.at[partner], p_recv.at[0])
    own = [part for h in halves for part in (choose(load(zbuf, g, h), t, g), choose(load(pbuf, partner, h), t, g))]
    own = term(own, g)
    arrived(tables.at[pl.ds(0, len(around))], t_recv)
    for h in halves:
        for k, j in enumerate(nearest):
            arrived(zbuf.at[j, h], z_recv.at[without(j, g), h])
            send(zbuf.at[j, h], xbuf.at[k, h], sent, x_recv, (partner, g))
            tiles = load(zbuf, j, h)
            for e, column in enumerate(around):
                sbuf[h, k, e] = choose(tiles, column, j)
            for e, column in enumerate(around):
                send(sbuf.at[h, k, e], abuf.at[h, k, t], sent, a_recv.at[h, without(place, rest[e // CORES])], (column, g))
    arrived(xbuf, x_recv)
    for h in halves:
        mine = [x[h * piece:(h + 1) * piece] for x in own]
        for k, j in enumerate(nearest):
            mine = add(mine, term([choose(load(zbuf, j, h), t, j), choose(load(xbuf, k, h), t, j)], j))
        finish(h, place, mine)

    arrived(pbuf.at[pl.ds(0, len(around))], p_recv.at[1])
    parts = [choose(load(pbuf, column, h), t, g) for h in halves for pair in columns for column in pair]
    base = term(parts, g)
    def turn(h, low, high):
        start = (h * len(rising) + low) * piece
        sums = [x[start:start + (high - low) * piece] for x in base]
        for where in rising[low:high]:
            arrived(abuf.at[h, :, pl.ds(0, CORES)], a_recv.at[h, without(where, place)])
        for k, j in enumerate(nearest):
            sums = add(sums, term([abuf[h, k, column] for pair in columns[low:high] for column in pair], j))
        for at in range(low, high):
            finish(h, rising[at], [x[(at - low) * piece:(at - low + 1) * piece] for x in sums])

    @pl.when(2 * g < groups)
    def _():
        for what in ((0, 0, 2), (0, 2, 3), (1, 0, 2), (1, 2, 3)):
            turn(*what)

    @pl.when(2 * g >= groups)
    def _():
        for what in ((0, 0, 1), (1, 0, 1), (0, 1, 2), (0, 2, 3), (1, 1, 2), (1, 2, 3)):
            turn(*what)

    first = core == 0
    for h in halves:
        total = acc[h, g]
        arrived(sums_buf.at[h, pl.ds(0, groups - 1)], rs_recv.at[h])
        for j in nearest:
            total = total + sums_buf[h, j].astype(jnp.float32)
        total = (0.5 * total).astype(out_ref.dtype)
        same, other = total[:pairs_dev], total[pairs_dev:]
        out_ref[h, :pairs_dev, :] = jnp.where(first, same, other)
        out_ref[h, pairs_dev:, :] = jnp.where(first, other, same)
    left(tables.at[pl.ds(0, len(around))], t_send)
    left(all_sent, sent)


def fused(groups, tiles, amplitudes, integrals, slot_cd, slot_ab):
    batch, pairs_dev, span = amplitudes.shape
    widths = integrals.shape[-1]
    places = tiles // CORES
    rows = pairs_dev * tiles // groups
    result = NT_DEV * widths
    tiles_dev = span // widths
    hbm = pl.BlockSpec(memory_space=pltpu.HBM)
    block = (batch, tiles_dev, pairs_dev, widths)
    piece = CORES * pairs_dev
    others, around = groups - 1, CORES * (places - 1)
    dma = pltpu.SemaphoreType.DMA
    all_sent = batch * ((2 * others + tiles - 1) * tiles_dev + others * around + others * CORES * NT_DEV)
    return pl.pallas_call(
        functools.partial(kernel, groups, places),
        out_shape=jax.ShapeDtypeStruct((batch, rows, result), jnp.bfloat16),
        in_specs=[hbm] * 4,
        out_specs=pl.BlockSpec(memory_space=pltpu.VMEM),
        scratch_shapes=[
            pltpu.VMEM((groups, *block), jnp.bfloat16),
            pltpu.VMEM((others, *block), jnp.bfloat16),
            pltpu.VMEM((tiles, *block), jnp.bfloat16),
            pltpu.VMEM((batch, others, tiles, pairs_dev, widths), jnp.bfloat16),
            pltpu.VMEM((batch, others, around, pairs_dev, widths), jnp.bfloat16),
            pltpu.VMEM(integrals.shape, jnp.bfloat16),
            pltpu.VMEM((batch, places, piece, result), jnp.float32),
            pltpu.VMEM((batch, places, piece, result), jnp.bfloat16),
            pltpu.VMEM((batch, groups, piece, result), jnp.bfloat16),
            pltpu.VMEM((all_sent, pairs_dev, widths), jnp.bfloat16),
            pltpu.SMEM((tiles + 1, *slot_cd.shape), jnp.int32),
            dma((3,)),
            dma,
            dma((others, batch)),
            dma,
            dma,
            dma((2,)),
            dma,
            dma((batch, places - 1)),
            dma((batch,)),
        ],
        compiler_params=pltpu.CompilerParams(collective_id=0, has_side_effects=True, vmem_limit_bytes=8 * 2**20),
    )(*(pltpu.with_memory_space_constraint(x, pltpu.HBM) for x in (amplitudes, integrals, slot_cd, slot_ab)))


def accumulate(slot_operands, slot_tiles, ab_list):
    row_count = slot_operands.shape[0]
    widths = slot_tiles.shape[-1]
    products = jnp.einsum(
        "rsc,scd->rsd", slot_operands, slot_tiles, preferred_element_type=jnp.float32
    )
    select = (ab_list[:, None] == jnp.arange(NT_DEV, dtype=jnp.int32)[None, :]).astype(jnp.float32)
    summed = jnp.einsum("rsd,sa->rad", products, select)
    return summed.reshape(row_count, NT_DEV * widths)


def by_slabs(amplitudes, integrals, slot_cd, slot_ab):
    groups = lax.axis_size("grp")
    own_index = lax.axis_index("grp")
    widths = integrals.shape[-1]
    pairs = amplitudes.shape[1] * lax.axis_size("tile")
    cd_table = slot_cd[0].reshape(groups, groups)
    ab_table = slot_ab[0].reshape(groups, groups)
    own_tiles = integrals[0]
    moved_tiles = lax.all_to_all(own_tiles, "grp", split_axis=0, concat_axis=0, tiled=True)
    cd_list = lax.dynamic_index_in_dim(cd_table, own_index, 1, keepdims=False)
    ab_list = lax.dynamic_index_in_dim(ab_table, own_index, 1, keepdims=False)
    outputs = []
    for batch_index in range(BATCH):
        slab_block = lax.all_gather(amplitudes[batch_index], "tile", axis=0, tiled=True)
        blocks = slab_block.reshape(pairs, slab_block.shape[1] // widths, widths)
        operands = jnp.take(blocks, cd_list, axis=1)
        full_terms = accumulate(operands, moved_tiles, ab_list)
        partial_value = lax.psum_scatter(full_terms, "grp", scatter_dimension=0, tiled=True)
        outputs.append((0.5 * partial_value).astype(jnp.bfloat16))
    return jnp.stack(outputs)


def solution(mesh):
    groups, tiles = mesh.shape["grp"], mesh.shape["tile"]

    def per_device(amplitudes, integrals, slot_cd, slot_ab):
        gathered = amplitudes.size * amplitudes.dtype.itemsize * groups * tiles
        if gathered > GATHER_LIMIT or tiles != CORES * groups or tiles & (tiles - 1):
            return by_slabs(amplitudes, integrals, slot_cd, slot_ab)
        return fused(groups, tiles, amplitudes, integrals, slot_cd, slot_ab)

    return jax.shard_map(
        per_device,
        mesh=mesh,
        in_specs=(
            P(None, "tile", "grp"),
            P("tile", "grp", None, None),
            P("tile", None),
            P("tile", None),
        ),
        out_specs=P(None, "grp", "tile"),
        check_vma=False,
    )
```
